32 devices in a mesh: dp: 2 (over core), expert: 16 (over z, y, x).
Axes of the slice: x: 2, y: 2, z: 4, core: 2. Of those that a mesh axis runs over, the one named last changes fastest.
Arguments:
- weights: bfloat16 [4, 3584, 512], P(None, ('dp', 'expert')), may hold values from -0.09375 to 0.09375
- first_moment: float32 [4, 3584, 512], P(None, ('dp', 'expert')), may hold values from -3 to 3
- second_moment: float32 [4, 3584, 512], P(None, ('dp', 'expert')), may hold values from 0.05 to 2
- placement: int32 [16], replicated, may hold values from 0 to 3, as said below
- block_counts: int32 [2, 16], P('dp', 'expert'), may hold values from 1 to 2
- tokens: bfloat16 [2, 16, 256, 3584], P('dp', 'expert'), may hold values from -6 to 6
- hidden_grad: bfloat16 [2, 16, 256, 256], P('dp', 'expert'), may hold values from -1.1953125 to 1.1953125
Outputs:
- new_weights: bfloat16 [16, 3584, 512], P('expert', 'dp')
- new_first: float32 [16, 3584, 512], P('expert', 'dp')
- new_second: float32 [16, 3584, 512], P('expert', 'dp')
The draws below stay inside these ranges and needn't reach their ends.
Inputs may be any that keep to these rules, and one draw needn't show every extreme that they name: `placement`: every expert block 0 to 3 is owned by at least one device. `block_counts`: the rows after a device's live blocks are padding.
All inputs are finite; a program needn't handle non-finite values.
Results may differ from the reference program's by a relative error of at most 0.015.
Values may be sent and summed in bfloat16 or wider, within the bound.
A program may use at most 64 MiB of HBM per device.

```python
import math
import jax
import jax.numpy as jnp
from jax import lax

D = 3584
FF_UNIT = 256
BLOCK = 128
MAX_BLOCKS = 2
ROWS = 256
UNITS = 4
N_DP = 2
N_EXPERT = 16


def draw_placement(key, part):
    folded = jax.random.fold_in(key, 17)
    key_first, key_second, key_blocks, key_devices = jax.random.split(folded, 4)
    first_draw = jax.random.randint(key_first, (N_EXPERT,), 0, UNITS)
    second_draw = jax.random.randint(key_second, (N_EXPERT,), 0, UNITS)
    skewed = first_draw * second_draw // UNITS
    device_slot = jnp.arange(N_EXPERT)
    chosen = jnp.where(device_slot < UNITS, device_slot, skewed)
    relabel = jax.random.permutation(key_blocks, UNITS)
    chosen = relabel[chosen]
    shuffle = jax.random.permutation(key_devices, N_EXPERT)
    return chosen[shuffle].astype(jnp.int32)


def plant(drawn, own_key, low, largest):
    spot = [jax.random.randint(jax.random.fold_in(own_key, axis), (), 0, length) for axis, length in enumerate(drawn.shape)]
    longest = drawn.shape.index(max(drawn.shape))
    beside = spot[:longest] + [(spot[longest] + 1) % drawn.shape[longest]] + spot[longest + 1:]
    return drawn.at[tuple(spot)].set(low).at[tuple(beside)].set(largest)


def levels(key, shape, cuts, low, largest):
    def one(dim, parts):
        heights = jax.random.uniform(jax.random.fold_in(jax.random.fold_in(key, 6), dim), (parts,), jnp.float32, low / len(cuts), largest / len(cuts))
        return jnp.repeat(jnp.exp(heights), shape[dim] // parts).reshape((-1,) + (1,) * (len(shape) - dim - 1))

    factor_of = one(*cuts[0])
    for cut in cuts[1:]:
        factor_of = factor_of * one(*cut)
    return factor_of


def gaussian(key, dims, scale, most, pieces=(), held_as=jnp.bfloat16):
    values = jax.random.normal(key, dims, jnp.float32) * scale
    if len(pieces) > 0:
        values = levels(key, dims, pieces, -0.22, 0.18) * values
    return jnp.clip(values, min=-most, max=most).astype(held_as)


def setup_inputs(seed: int = 0) -> dict:
    streams_of = jax.random.split(jax.random.key(seed), 8)
    return {
        "weights": gaussian(streams_of[0], (UNITS, D, 2 * FF_UNIT), D ** -0.5, 0.09375, ((1, 32),)),
        "first_moment": gaussian(streams_of[1], (UNITS, D, 2 * FF_UNIT), 0.5, 3.0, ((1, 32),), jnp.float32),
        "second_moment": jnp.clip(jnp.exp(math.log(2.0) - 3.6888794 * jax.random.uniform(streams_of[2], (UNITS, D, 2 * FF_UNIT), jnp.float32) ** levels(streams_of[2], (UNITS, D, 2 * FF_UNIT), ((1, 32),), -0.2, 0.2)), 0.05, 2.0),
        "placement": draw_placement(jax.random.fold_in(streams_of[7], 71), 0),
        "block_counts": plant(jax.random.randint(streams_of[4], (N_DP, N_EXPERT), 1, MAX_BLOCKS + 1), jax.random.fold_in(streams_of[4], 1), 1, MAX_BLOCKS).astype(jnp.int32),
        "tokens": gaussian(streams_of[5], (N_DP, N_EXPERT, ROWS, D), 1.0, 6.0, ((0, 2), (1, 16))),
        "hidden_grad": gaussian(streams_of[6], (N_DP, N_EXPERT, ROWS, FF_UNIT), 0.2, 1.1953125, ((0, 2), (1, 16))),
    }


beta_first = 0.9
beta_second = 0.95
learning_rate = 0.001
weight_decay = 0.1
adam_epsilon = 1e-08
adam_steps = 10.0

def silu_grads(projected, upstream, live_mask):
    half_width = projected.shape[1] // 2
    gate_part = projected[:, :half_width]
    upward = projected[:, half_width:]
    sigmoid_gate = jax.nn.sigmoid(gate_part)
    masked = jnp.where(live_mask, upstream.astype(jnp.float32), 0.0)
    grad_gate = masked * upward * sigmoid_gate * (1.0 + gate_part * (1.0 - sigmoid_gate))
    grad_upward = masked * gate_part * sigmoid_gate
    return jnp.concatenate([grad_gate, grad_upward], axis=1).astype(jnp.bfloat16)

def adam_update(params, first_moment, second_moment, gradient):
    moment_one = beta_first * first_moment + (1.0 - beta_first) * gradient
    moment_two = beta_second * second_moment + (1.0 - beta_second) * gradient * gradient
    correct_one = 1.0 - beta_first ** adam_steps
    correct_two = 1.0 - beta_second ** adam_steps
    params_full = params.astype(jnp.float32)
    step_size = moment_one / correct_one / (jnp.sqrt(moment_two / correct_two) + adam_epsilon) + weight_decay * params_full
    return ((params_full - learning_rate * step_size).astype(jnp.bfloat16), moment_one, moment_two)

def reference(weights, first_moment, second_moment, placement, block_counts, tokens, hidden_grad):
    dev_tokens = tokens.reshape(N_DP * N_EXPERT, ROWS, D)
    dev_grads = hidden_grad.reshape(N_DP * N_EXPERT, ROWS, FF_UNIT)
    dev_counts = block_counts.reshape(N_DP * N_EXPERT)
    dev_blocks = jnp.tile(placement, N_DP)

    def accumulate(summed, device_item):
        inputs, upstream, counted, block_id = device_item
        matrix = lax.dynamic_index_in_dim(weights, block_id, 0, keepdims=False)
        projected = jnp.dot(inputs, matrix, preferred_element_type=jnp.float32)
        live_mask = (jnp.arange(ROWS) < BLOCK * counted)[:, None]
        grad_proj = silu_grads(projected, upstream, live_mask)
        local_grad = jnp.dot(inputs.T, grad_proj, preferred_element_type=jnp.float32).astype(jnp.bfloat16)
        local_grad = lax.optimization_barrier(local_grad).astype(jnp.float32)
        return (summed.at[block_id].add(local_grad), None)
    zero_grads = jnp.zeros((UNITS, D, 2 * FF_UNIT), jnp.float32)
    gradient = lax.scan(accumulate, zero_grads, (dev_tokens, dev_grads, dev_counts, dev_blocks))[0]
    updated, moment_one, moment_two = adam_update(weights, first_moment, second_moment, gradient)
    return (jnp.take(updated, placement, axis=0), jnp.take(moment_one, placement, axis=0), jnp.take(moment_two, placement, axis=0))
```

```python
import jax
import jax.numpy as jnp
from jax import lax
from jax.sharding import PartitionSpec as P

BLOCK = 128


beta_first = 0.9
beta_second = 0.95
learning_rate = 0.001
weight_decay = 0.1
adam_epsilon = 1e-08
adam_steps = 10.0


def silu_grads(projected, upstream, live_mask):
    half_width = projected.shape[1] // 2
    gate_part = projected[:, :half_width]
    upward = projected[:, half_width:]
    sigmoid_gate = jax.nn.sigmoid(gate_part)
    masked = jnp.where(live_mask, upstream.astype(jnp.float32), 0.0)
    grad_gate = masked * upward * sigmoid_gate * (1.0 + gate_part * (1.0 - sigmoid_gate))
    grad_upward = masked * gate_part * sigmoid_gate
    return jnp.concatenate([grad_gate, grad_upward], axis=1).astype(jnp.bfloat16)


def moments(first_moment, second_moment, gradient):
    moment_one = beta_first * first_moment + (1.0 - beta_first) * gradient
    moment_two = beta_second * second_moment + (1.0 - beta_second) * gradient * gradient
    return moment_one, moment_two


def new_params(params, moment_one, moment_two):
    correct_one = 1.0 - beta_first**adam_steps
    correct_two = 1.0 - beta_second**adam_steps
    params_full = params.astype(jnp.float32)
    step_size = (
        moment_one / correct_one / (jnp.sqrt(moment_two / correct_two) + adam_epsilon)
        + weight_decay * params_full
    )
    return (params_full - learning_rate * step_size).astype(jnp.bfloat16)


def exchange(x, axis):
    return lax.all_to_all(x, axis, split_axis=0, concat_axis=0, tiled=True)


def on_device(weights, first_moment, second_moment, placement, block_counts, tokens, hidden_grad):
    expert_count = lax.axis_size("expert")
    dp_count = lax.axis_size("dp")
    block_total, span_rows, col_total = weights.shape
    row_total = tokens.shape[2]
    part_rows = expert_count * span_rows
    owner_table = (placement[:, None] == jnp.arange(block_total)[None, :]).astype(jnp.bfloat16)
    live_mask = (jnp.arange(row_total) < BLOCK * block_counts[0, 0])[:, None]

    own_rows = exchange(jnp.take(weights, placement, axis=0), "expert")
    own_rows = own_rows.reshape(part_rows, col_total)
    inputs = lax.all_to_all(tokens[0, 0], "dp", split_axis=1, concat_axis=0, tiled=True)
    partial = jnp.dot(inputs, own_rows, preferred_element_type=jnp.float32)
    projected = lax.psum_scatter(partial, "dp", scatter_dimension=0, tiled=True)
    grad_proj = silu_grads(projected, hidden_grad[0, 0], live_mask)
    grad_proj = lax.all_gather(grad_proj, "dp", axis=0, tiled=True)
    term = lax.dot_general(
        inputs, grad_proj, (((0,), (0,)), ((), ())), preferred_element_type=jnp.float32
    ).astype(jnp.bfloat16)
    at_home = exchange(term.reshape(expert_count, span_rows * col_total), "expert")
    block_grad = lax.dot_general(
        owner_table, at_home, (((0,), (0,)), ((), ())), preferred_element_type=jnp.float32
    ).reshape(block_total, span_rows, col_total)
    moment_one, moment_two = moments(first_moment, second_moment, block_grad)
    one_here = exchange(jnp.take(moment_one.astype(jnp.bfloat16), placement, axis=0), "expert")
    two_here = exchange(jnp.take(moment_two.astype(jnp.bfloat16), placement, axis=0), "expert")
    one_here = one_here.reshape(part_rows, col_total).astype(jnp.float32)
    two_here = two_here.reshape(part_rows, col_total).astype(jnp.float32)
    updated = new_params(own_rows, one_here, two_here)
    return (updated[None], one_here[None], two_here[None])


def solution(mesh):
    in_specs = (
        P(None, ("dp", "expert"), None),
        P(None, ("dp", "expert"), None),
        P(None, ("dp", "expert"), None),
        P(),
        P("dp", "expert"),
        P("dp", "expert", None, None),
        P("dp", "expert", None, None),
    )
    out_specs = (P("expert", "dp", None), P("expert", "dp", None), P("expert", "dp", None))
    return jax.shard_map(
        on_device, mesh=mesh, in_specs=in_specs, out_specs=out_specs, check_vma=False
    )
```

```python
import functools

import jax
import jax.numpy as jnp
from jax import lax
from jax.experimental import pallas as pl
from jax.experimental.pallas import tpu as pltpu
from jax.sharding import PartitionSpec as P

BLOCK = 128


beta_first = 0.9
beta_second = 0.95
learning_rate = 0.001
weight_decay = 0.1
adam_epsilon = 1e-08
adam_steps = 10.0


def silu_grads(projected, upstream, live_mask):
    half_width = projected.shape[1] // 2
    gate_part = projected[:, :half_width]
    upward = projected[:, half_width:]
    sigmoid_gate = jax.nn.sigmoid(gate_part)
    masked = jnp.where(live_mask, upstream.astype(jnp.float32), 0.0)
    grad_gate = masked * upward * sigmoid_gate * (1.0 + gate_part * (1.0 - sigmoid_gate))
    grad_upward = masked * gate_part * sigmoid_gate
    return jnp.concatenate([grad_gate, grad_upward], axis=1).astype(jnp.bfloat16)


def moments(first_moment, second_moment, gradient):
    moment_one = beta_first * first_moment + (1.0 - beta_first) * gradient
    moment_two = beta_second * second_moment + (1.0 - beta_second) * gradient * gradient
    return moment_one, moment_two


def new_params(params, moment_one, moment_two):
    correct_one = 1.0 - beta_first**adam_steps
    correct_two = 1.0 - beta_second**adam_steps
    params_full = params.astype(jnp.float32)
    step_size = (
        moment_one / correct_one / (jnp.sqrt(moment_two / correct_two) + adam_epsilon)
        + weight_decay * params_full
    )
    return (params_full - learning_rate * step_size).astype(jnp.bfloat16)


def exchange(x, axis):
    return lax.all_to_all(x, axis, split_axis=0, concat_axis=0, tiled=True)


def on_device_wide(weights, first_moment, second_moment, placement, block_counts, tokens, hidden_grad):
    expert_count = lax.axis_size("expert")
    dp_count = lax.axis_size("dp")
    block_total, span_rows, col_total = weights.shape
    row_total = tokens.shape[2]
    part_rows = expert_count * span_rows
    owner_table = (placement[:, None] == jnp.arange(block_total)[None, :]).astype(jnp.bfloat16)
    live_mask = (jnp.arange(row_total) < BLOCK * block_counts[0, 0])[:, None]

    own_rows = exchange(jnp.take(weights, placement, axis=0), "expert")
    own_rows = own_rows.reshape(part_rows, col_total)
    inputs = lax.all_to_all(tokens[0, 0], "dp", split_axis=1, concat_axis=0, tiled=True)
    partial = jnp.dot(inputs, own_rows, preferred_element_type=jnp.float32)
    projected = lax.psum_scatter(partial, "dp", scatter_dimension=0, tiled=True)
    grad_proj = silu_grads(projected, hidden_grad[0, 0], live_mask)
    grad_proj = lax.all_gather(grad_proj, "dp", axis=0, tiled=True)
    term = lax.dot_general(
        inputs, grad_proj, (((0,), (0,)), ((), ())), preferred_element_type=jnp.float32
    ).astype(jnp.bfloat16)
    at_home = exchange(term.reshape(expert_count, span_rows * col_total), "expert")
    block_grad = lax.dot_general(
        owner_table, at_home, (((0,), (0,)), ((), ())), preferred_element_type=jnp.float32
    ).reshape(block_total, span_rows, col_total)
    moment_one, moment_two = moments(first_moment, second_moment, block_grad)
    one_here = exchange(jnp.take(moment_one.astype(jnp.bfloat16), placement, axis=0), "expert")
    two_here = exchange(jnp.take(moment_two.astype(jnp.bfloat16), placement, axis=0), "expert")
    one_here = one_here.reshape(part_rows, col_total).astype(jnp.float32)
    two_here = two_here.reshape(part_rows, col_total).astype(jnp.float32)
    updated = new_params(own_rows, one_here, two_here)
    return (updated[None], one_here[None], two_here[None])


MESH = pl.DeviceIdType.MESH
VMEM_BYTES = 60 * 1024 * 1024


def plane_size(expert_count):
    size = 1
    while 4 * size * size <= expert_count:
        size *= 2
    return size


def remote(source, target, send_sem, recv_sem, axis, index):
    return pltpu.make_async_remote_copy(
        src_ref=source, dst_ref=target, send_sem=send_sem, recv_sem=recv_sem,
        device_id={axis: index}, device_id_type=MESH,
    )


def greet(level, levels, near, me, with_dp):
    barrier = pltpu.get_barrier_semaphore()

    def signal(axis, index):
        pl.semaphore_signal(barrier, inc=1, device_id={axis: index}, device_id_type=MESH)

    for step in range(1, near):
        signal("expert", me - me % near + ((me % near) ^ step))
    if with_dp:
        signal("dp", 1 - lax.axis_index("dp"))
    pl.when(level > 0)(lambda: signal("expert", me - near))
    pl.when(level < levels - 1)(lambda: signal("expert", me + near))
    count = near - 1 + int(with_dp)
    pl.semaphore_wait(
        barrier, count + (level > 0).astype(jnp.int32) + (level < levels - 1).astype(jnp.int32)
    )


def gather_kernel(channels, levels, near, with_tokens, *refs):
    slots = channels * (levels - 1)
    fixed = 5 if with_tokens else 3
    from_below, from_above = refs[fixed:fixed + slots], refs[fixed + slots:fixed + 2 * slots]
    refs = refs[:fixed] + refs[fixed + 2 * slots:]

    def slot(channel, hop):
        return channel * (levels - 1) + hop

    if with_tokens:
        (place, slab, tokens, out, inputs, chosen,
         up_send, up_recv, down_send, down_recv, near_send, near_recv, dp_send, dp_recv, own_sem) = refs
    else:
        (place, slab, out, chosen,
         up_send, up_recv, down_send, down_recv, near_send, near_recv) = refs
    me = lax.axis_index("expert")
    level, spot = me // near, me % near
    greet(level, levels, near, me, with_tokens)

    def up(channel, hop):
        source = slab.at[channel] if hop == 0 else from_below[slot(channel, hop - 1)]
        return remote(source, from_below[slot(channel, hop)], up_send.at[channel, hop],
                      up_recv.at[channel, hop], "expert", me + near)

    def down(channel, hop):
        source = slab.at[channel] if hop == 0 else from_above[slot(channel, hop - 1)]
        return remote(source, from_above[slot(channel, hop)], down_send.at[channel, hop],
                      down_recv.at[channel, hop], "expert", me - near)

    def across(channel, origin, step):
        return remote(chosen.at[channel, origin, step - 1], out.at[channel, origin, spot],
                      near_send.at[channel, origin, step - 1], near_recv.at[channel, origin, step - 1],
                      "expert", level * near + (spot ^ step))

    def hand_on(channel, origin, held):
        for step in range(1, near):
            chosen[channel, origin, step - 1] = held[place[level * near + (spot ^ step)]]
            across(channel, origin, step).start()
        out[channel, origin, spot] = held[place[me]]

    for channel in range(channels):
        pl.when(level < levels - 1)(lambda c=channel: up(c, 0).start())
        pl.when(level > 0)(lambda c=channel: down(c, 0).start())
    if with_tokens:
        core = lax.axis_index("dp")
        width = inputs.shape[2]
        other = 1 - core

        def columns(index):
            return tokens.at[:, pl.ds(pl.multiple_of(index * width, 128), width)]

        swap = remote(columns(other), inputs.at[core], dp_send, dp_recv, "dp", other)
        swap.start()
        keep = pltpu.make_async_copy(columns(core), inputs.at[core], own_sem)
        keep.start()
    for channel in range(channels):
        hand_on(channel, level, slab.at[channel])
    for hop in range(levels - 1):
        for channel in range(channels):

            @pl.when(level > hop)
            def _():
                up(channel, hop).wait_recv()
                if hop < levels - 2:
                    pl.when(level < levels - 1)(lambda: up(channel, hop + 1).start())
                hand_on(channel, level - hop - 1, from_below[slot(channel, hop)])

            @pl.when(level < levels - 1 - hop)
            def _():
                down(channel, hop).wait_recv()
                if hop < levels - 2:
                    pl.when(level > 0)(lambda: down(channel, hop + 1).start())
                hand_on(channel, level + hop + 1, from_above[slot(channel, hop)])

    for channel in range(channels):
        for hop in range(levels - 1):
            pl.when((level < levels - 1) & (level >= hop))(lambda c=channel, h=hop: up(c, h).wait_send())
            pl.when((level > 0) & (level < levels - hop))(lambda c=channel, h=hop: down(c, h).wait_send())
        for origin in range(levels):
            for step in range(1, near):
                across(channel, origin, step).wait()
    if with_tokens:
        swap.wait()
        keep.wait()


def reduce_kernel(levels, near, place, term, out, arrived, below, above, to_up, to_down,
                  up_send, up_recv, down_send, down_recv, near_send, near_recv):
    me = lax.axis_index("expert")
    level, spot = me // near, me % near
    blocks, rows, cols = out.shape
    greet(level, levels, near, me, False)

    def across(goal, step):
        return remote(term.at[goal, spot ^ step], arrived.at[goal, step - 1],
                      near_send.at[goal, step - 1], near_recv.at[goal, step - 1],
                      "expert", level * near + (spot ^ step))

    def up(left):
        return remote(to_up.at[left - 1], below.at[left - 1], up_send.at[left - 1],
                      up_recv.at[left - 1], "expert", me + near)

    def down(left):
        return remote(to_down.at[left - 1], above.at[left - 1], down_send.at[left - 1],
                      down_recv.at[left - 1], "expert", me - near)

    def start_near(goal):
        for step in range(1, near):
            across(goal, step).start()

    def sums(goal, target, extra):
        for step in range(1, near):
            across(goal, step).wait_recv()
        owners = [place[level * near + (spot ^ step)] for step in range(near)]

        @pl.loop(0, rows // 16)
        def _(tile):
            here = pl.ds(pl.multiple_of(tile * 16, 16), 16)
            terms = [term[goal, spot, here, :].astype(jnp.float32)]
            terms += [arrived[goal, step - 1, here, :].astype(jnp.float32) for step in range(1, near)]
            for block in range(blocks):
                total = None
                for owner, value in zip(owners, terms):
                    part = jnp.where(owner == block, 1.0, 0.0) * value
                    total = part if total is None else total + part
                for ref in extra:
                    total = total + ref[block, here, :].astype(jnp.float32)
                target[block, here, :] = total.astype(target.dtype)

    for left in range(levels - 1, 0, -1):
        pl.when(level + left < levels)(lambda n=left: start_near(level + n))
        pl.when(level >= left)(lambda n=left: start_near(level - n))
    start_near(level)
    for left in range(levels - 1, 0, -1):

        @pl.when(level + left < levels)
        def _():
            if left < levels - 1:
                @pl.when(level > 0)
                def _():
                    up(left + 1).wait_recv()
                    sums(level + left, to_up.at[left - 1], [below.at[left]])

            @pl.when(level == 0)
            def _():
                sums(level + left, to_up.at[left - 1], [])

            up(left).start()

        @pl.when(level >= left)
        def _():
            if left < levels - 1:
                @pl.when(level < levels - 1)
                def _():
                    down(left + 1).wait_recv()
                    sums(level - left, to_down.at[left - 1], [above.at[left]])

            @pl.when(level == levels - 1)
            def _():
                sums(level - left, to_down.at[left - 1], [])

            down(left).start()

    sums(level, out, [])

    def add(ref):
        @pl.loop(0, rows // 16)
        def _(tile):
            here = pl.ds(pl.multiple_of(tile * 16, 16), 16)
            for block in range(blocks):
                out[block, here, :] += ref[block, here, :].astype(jnp.float32)

    @pl.when(level > 0)
    def _():
        up(1).wait_recv()
        add(below.at[0])

    @pl.when(level < levels - 1)
    def _():
        down(1).wait_recv()
        add(above.at[0])

    for left in range(1, levels):
        pl.when(level + left < levels)(lambda n=left: up(n).wait_send())
        pl.when(level >= left)(lambda n=left: down(n).wait_send())
    for goal in range(levels):
        for step in range(1, near):
            across(goal, step).wait_send()


def in_vmem():
    return pl.BlockSpec(memory_space=pltpu.VMEM)


def in_smem():
    return pl.BlockSpec(memory_space=pltpu.SMEM)


def call_gather(placement, slab, levels, near, collective_id, tokens=None):
    channels, blocks, rows, cols = slab.shape
    kind = slab.dtype
    out_shape = [jax.ShapeDtypeStruct((channels, levels, near, rows, cols), kind)]
    in_specs = [in_smem(), in_vmem()]
    operands = [placement, slab]
    out_specs = [in_vmem()]
    dma = pltpu.SemaphoreType.DMA
    scratch = [pltpu.VMEM((blocks, rows, cols), kind)] * (2 * channels * (levels - 1))
    scratch += [pltpu.VMEM((channels, levels, near - 1, rows, cols), kind)]
    scratch += [dma((channels, levels - 1))] * 4 + [dma((channels, levels, near - 1))] * 2
    if tokens is not None:
        count, width = tokens.shape
        out_shape.append(jax.ShapeDtypeStruct((2, count, width // 2), tokens.dtype))
        in_specs.append(in_vmem())
        operands.append(tokens)
        out_specs.append(in_vmem())
        scratch += [dma, dma, dma]
    return pl.pallas_call(
        functools.partial(gather_kernel, channels, levels, near, tokens is not None),
        out_shape=out_shape, in_specs=in_specs, out_specs=out_specs, scratch_shapes=scratch,
        compiler_params=pltpu.CompilerParams(
            collective_id=collective_id, has_side_effects=True, vmem_limit_bytes=VMEM_BYTES
        ),
    )(*operands)


def call_reduce(placement, term, blocks, collective_id):
    levels, near, rows, cols = term.shape
    kind = term.dtype
    dma = pltpu.SemaphoreType.DMA
    return pl.pallas_call(
        functools.partial(reduce_kernel, levels, near),
        out_shape=jax.ShapeDtypeStruct((blocks, rows, cols), jnp.float32),
        in_specs=[in_smem(), in_vmem()], out_specs=in_vmem(),
        scratch_shapes=[pltpu.VMEM((levels, near - 1, rows, cols), kind)]
        + [pltpu.VMEM((levels - 1, blocks, rows, cols), kind)] * 4
        + [dma((levels - 1,))] * 4 + [dma((levels, near - 1))] * 2,
        compiler_params=pltpu.CompilerParams(
            collective_id=collective_id, has_side_effects=True, vmem_limit_bytes=VMEM_BYTES
        ),
    )(placement, term)


def on_device(weights, first_moment, second_moment, placement, block_counts, tokens, hidden_grad):
    expert_count = lax.axis_size("expert")
    dp_count = lax.axis_size("dp")
    block_total, span_rows, col_total = weights.shape
    row_total, model = tokens.shape[2:]
    near = plane_size(expert_count)
    levels = expert_count // near
    fits = dp_count == 2 and near > 1 and levels > 1 and levels * near == expert_count
    if not fits or span_rows % 16 or model % 256 or col_total % 128 or row_total % 16:
        return on_device_wide(
            weights, first_moment, second_moment, placement, block_counts, tokens, hidden_grad
        )
    part_rows = expert_count * span_rows
    core = lax.axis_index("dp")
    swap = [(0, 1), (1, 0)]
    live_mask = (jnp.arange(row_total) < BLOCK * block_counts[0, 0])[:, None]

    own_rows, inputs = call_gather(placement, weights[None], levels, near, 0, tokens[0, 0])
    own_rows = own_rows.reshape(part_rows, col_total)
    inputs = inputs.reshape(2 * row_total, model // 2)
    mine = lax.dynamic_slice_in_dim(inputs, core * row_total, row_total)
    others = lax.dynamic_slice_in_dim(inputs, (1 - core) * row_total, row_total)
    away = jnp.dot(others, own_rows, preferred_element_type=jnp.float32)
    away = lax.ppermute(away, "dp", swap)
    projected = jnp.dot(mine, own_rows, preferred_element_type=jnp.float32) + away
    grad_here = silu_grads(projected, hidden_grad[0, 0], live_mask)
    grad_away = lax.ppermute(grad_here, "dp", swap)
    down = (((0,), (0,)), ((), ()))
    ordered = jnp.where(core == 0, jnp.stack([grad_here, grad_away]), jnp.stack([grad_away, grad_here]))
    term = lax.dot_general(
        inputs, ordered.reshape(2 * row_total, col_total), down, preferred_element_type=jnp.float32
    ).astype(jnp.bfloat16)
    block_grad = call_reduce(
        placement, term.reshape(levels, near, span_rows, col_total), block_total, 1
    )
    moment_one, moment_two = moments(first_moment, second_moment, block_grad)
    both = jnp.stack([moment_one.astype(jnp.bfloat16), moment_two.astype(jnp.bfloat16)])
    (here,) = call_gather(placement, both, levels, near, 2)
    here = here.reshape(2, part_rows, col_total).astype(jnp.float32)
    updated = new_params(own_rows, here[0], here[1])
    return (updated[None], here[0][None], here[1][None])


def solution(mesh):
    in_specs = (
        P(None, ("dp", "expert"), None),
        P(None, ("dp", "expert"), None),
        P(None, ("dp", "expert"), None),
        P(),
        P("dp", "expert"),
        P("dp", "expert", None, None),
        P("dp", "expert", None, None),
    )
    out_specs = (P("expert", "dp", None), P("expert", "dp", None), P("expert", "dp", None))
    return jax.shard_map(
        on_device, mesh=mesh, in_specs=in_specs, out_specs=out_specs, check_vma=False
    )
```

```python
import functools

import jax
import jax.numpy as jnp
from jax import lax
from jax.experimental import pallas as pl
from jax.experimental.pallas import tpu as pltpu
from jax.sharding import PartitionSpec as P

BLOCK = 128


beta_first = 0.9
beta_second = 0.95
learning_rate = 0.001
weight_decay = 0.1
adam_epsilon = 1e-08
adam_steps = 10.0


def silu_grads(projected, upstream, live_mask):
    half_width = projected.shape[1] // 2
    gate_part = projected[:, :half_width]
    upward = projected[:, half_width:]
    sigmoid_gate = jax.nn.sigmoid(gate_part)
    masked = jnp.where(live_mask, upstream.astype(jnp.float32), 0.0)
    grad_gate = masked * upward * sigmoid_gate * (1.0 + gate_part * (1.0 - sigmoid_gate))
    grad_upward = masked * gate_part * sigmoid_gate
    return jnp.concatenate([grad_gate, grad_upward], axis=1).astype(jnp.bfloat16)


def moments(first_moment, second_moment, gradient):
    moment_one = beta_first * first_moment + (1.0 - beta_first) * gradient
    moment_two = beta_second * second_moment + (1.0 - beta_second) * gradient * gradient
    return moment_one, moment_two


def new_params(params, moment_one, moment_two):
    correct_one = 1.0 - beta_first**adam_steps
    correct_two = 1.0 - beta_second**adam_steps
    params_full = params.astype(jnp.float32)
    step_size = (
        moment_one / correct_one / (jnp.sqrt(moment_two / correct_two) + adam_epsilon)
        + weight_decay * params_full
    )
    return (params_full - learning_rate * step_size).astype(jnp.bfloat16)


def exchange(x, axis):
    return lax.all_to_all(x, axis, split_axis=0, concat_axis=0, tiled=True)


def on_device_wide(weights, first_moment, second_moment, placement, block_counts, tokens, hidden_grad):
    expert_count = lax.axis_size("expert")
    dp_count = lax.axis_size("dp")
    block_total, span_rows, col_total = weights.shape
    row_total = tokens.shape[2]
    part_rows = expert_count * span_rows
    owner_table = (placement[:, None] == jnp.arange(block_total)[None, :]).astype(jnp.bfloat16)
    live_mask = (jnp.arange(row_total) < BLOCK * block_counts[0, 0])[:, None]

    own_rows = exchange(jnp.take(weights, placement, axis=0), "expert")
    own_rows = own_rows.reshape(part_rows, col_total)
    inputs = lax.all_to_all(tokens[0, 0], "dp", split_axis=1, concat_axis=0, tiled=True)
    partial = jnp.dot(inputs, own_rows, preferred_element_type=jnp.float32)
    projected = lax.psum_scatter(partial, "dp", scatter_dimension=0, tiled=True)
    grad_proj = silu_grads(projected, hidden_grad[0, 0], live_mask)
    grad_proj = lax.all_gather(grad_proj, "dp", axis=0, tiled=True)
    term = lax.dot_general(
        inputs, grad_proj, (((0,), (0,)), ((), ())), preferred_element_type=jnp.float32
    ).astype(jnp.bfloat16)
    at_home = exchange(term.reshape(expert_count, span_rows * col_total), "expert")
    block_grad = lax.dot_general(
        owner_table, at_home, (((0,), (0,)), ((), ())), preferred_element_type=jnp.float32
    ).reshape(block_total, span_rows, col_total)
    moment_one, moment_two = moments(first_moment, second_moment, block_grad)
    one_here = exchange(jnp.take(moment_one.astype(jnp.bfloat16), placement, axis=0), "expert")
    two_here = exchange(jnp.take(moment_two.astype(jnp.bfloat16), placement, axis=0), "expert")
    one_here = one_here.reshape(part_rows, col_total).astype(jnp.float32)
    two_here = two_here.reshape(part_rows, col_total).astype(jnp.float32)
    updated = new_params(own_rows, one_here, two_here)
    return (updated[None], one_here[None], two_here[None])


MESH = pl.DeviceIdType.MESH
VMEM_BYTES = 60 * 1024 * 1024
PIECES = 2


def plane_size(expert_count):
    size = 1
    while 4 * size * size <= expert_count:
        size *= 2
    return size


def remote(source, target, send_sem, recv_sem, axis, index):
    return pltpu.make_async_remote_copy(
        src_ref=source, dst_ref=target, send_sem=send_sem, recv_sem=recv_sem,
        device_id={axis: index}, device_id_type=MESH,
    )


def greet(level, levels, near, me, with_dp):
    barrier = pltpu.get_barrier_semaphore()

    def signal(axis, index):
        pl.semaphore_signal(barrier, inc=1, device_id={axis: index}, device_id_type=MESH)

    for step in range(1, near):
        signal("expert", me - me % near + ((me % near) ^ step))
    if with_dp:
        signal("dp", 1 - lax.axis_index("dp"))
    pl.when(level > 0)(lambda: signal("expert", me - near))
    pl.when(level < levels - 1)(lambda: signal("expert", me + near))
    count = near - 1 + int(with_dp)
    pl.semaphore_wait(
        barrier, count + (level > 0).astype(jnp.int32) + (level < levels - 1).astype(jnp.int32)
    )


def gather_kernel(channels, levels, near, with_tokens, *refs):
    slots = channels * (levels - 1)
    fixed = 5 if with_tokens else 3
    from_below, from_above = refs[fixed:fixed + slots], refs[fixed + slots:fixed + 2 * slots]
    refs = refs[:fixed] + refs[fixed + 2 * slots:]

    def slot(channel, hop):
        return channel * (levels - 1) + hop

    if with_tokens:
        (place, slab, tokens, out, inputs, chosen,
         up_send, up_recv, down_send, down_recv, near_send, near_recv, dp_send, dp_recv, own_sem) = refs
    else:
        (place, slab, out, chosen,
         up_send, up_recv, down_send, down_recv, near_send, near_recv) = refs
    me = lax.axis_index("expert")
    level, spot = me // near, me % near
    greet(level, levels, near, me, with_tokens)

    def up(channel, hop):
        source = slab.at[channel] if hop == 0 else from_below[slot(channel, hop - 1)]
        return remote(source, from_below[slot(channel, hop)], up_send.at[channel, hop],
                      up_recv.at[channel, hop], "expert", me + near)

    def down(channel, hop):
        source = slab.at[channel] if hop == 0 else from_above[slot(channel, hop - 1)]
        return remote(source, from_above[slot(channel, hop)], down_send.at[channel, hop],
                      down_recv.at[channel, hop], "expert", me - near)

    def across(channel, origin, step):
        return remote(chosen.at[channel, origin, step - 1], out.at[channel, origin, spot],
                      near_send.at[channel, origin, step - 1], near_recv.at[channel, origin, step - 1],
                      "expert", level * near + (spot ^ step))

    def hand_on(channel, origin, held):
        for step in range(1, near):
            chosen[channel, origin, step - 1] = held[place[level * near + (spot ^ step)]]
            across(channel, origin, step).start()
        out[channel, origin, spot] = held[place[me]]

    for channel in range(channels):
        pl.when(level < levels - 1)(lambda c=channel: up(c, 0).start())
        pl.when(level > 0)(lambda c=channel: down(c, 0).start())
    if with_tokens:
        core = lax.axis_index("dp")
        width = inputs.shape[2]
        other = 1 - core

        def columns(index):
            return tokens.at[:, pl.ds(pl.multiple_of(index * width, 128), width)]

        swap = remote(columns(other), inputs.at[core], dp_send, dp_recv, "dp", other)
        swap.start()
        keep = pltpu.make_async_copy(columns(core), inputs.at[core], own_sem)
        keep.start()
    for channel in range(channels):
        hand_on(channel, level, slab.at[channel])
    for hop in range(levels - 1):
        for channel in range(channels):

            @pl.when(level > hop)
            def _():
                up(channel, hop).wait_recv()
                if hop < levels - 2:
                    pl.when(level < levels - 1)(lambda: up(channel, hop + 1).start())
                hand_on(channel, level - hop - 1, from_below[slot(channel, hop)])

            @pl.when(level < levels - 1 - hop)
            def _():
                down(channel, hop).wait_recv()
                if hop < levels - 2:
                    pl.when(level > 0)(lambda: down(channel, hop + 1).start())
                hand_on(channel, level + hop + 1, from_above[slot(channel, hop)])

    for channel in range(channels):
        for hop in range(levels - 1):
            pl.when((level < levels - 1) & (level >= hop))(lambda c=channel, h=hop: up(c, h).wait_send())
            pl.when((level > 0) & (level < levels - hop))(lambda c=channel, h=hop: down(c, h).wait_send())
        for origin in range(levels):
            for step in range(1, near):
                across(channel, origin, step).wait()
    if with_tokens:
        swap.wait()
        keep.wait()


def update_kernel(levels, near, cuts, *refs):
    place, term, first, second, out = refs[:5]
    chunks, hops = len(cuts), levels - 1
    at = [5]

    def take(count):
        at[0] += count
        return refs[at[0] - count:at[0]]

    arrived, below, above, to_up, to_down, slabs, picked = (take(chunks) for _ in range(7))
    from_below, from_above = take(chunks * hops), take(chunks * hops)
    (sum_up_send, sum_up_recv, sum_down_send, sum_down_recv, sum_near_send, sum_near_recv,
     up_send, up_recv, down_send, down_recv, near_send, near_recv) = refs[at[0]:]
    me = lax.axis_index("expert")
    level, spot = me // near, me % near
    blocks, _, cols = first.shape
    starts = [sum(cuts[:chunk]) for chunk in range(chunks)]
    greet(level, levels, near, me, False)

    def sum_across(chunk, goal, step):
        rows = pl.ds(starts[chunk], cuts[chunk])
        return remote(term.at[goal, spot ^ step, rows], arrived[chunk].at[goal, step - 1],
                      sum_near_send.at[chunk, goal, step - 1], sum_near_recv.at[chunk, goal, step - 1],
                      "expert", level * near + (spot ^ step))

    def sum_up(chunk, left):
        return remote(to_up[chunk].at[left - 1], below[chunk].at[left - 1], sum_up_send.at[chunk, left - 1],
                      sum_up_recv.at[chunk, left - 1], "expert", me + near)

    def sum_down(chunk, left):
        return remote(to_down[chunk].at[left - 1], above[chunk].at[left - 1],
                      sum_down_send.at[chunk, left - 1], sum_down_recv.at[chunk, left - 1],
                      "expert", me - near)

    def sum_start(chunk, goal):
        for step in range(1, near):
            sum_across(chunk, goal, step).start()

    def sums(chunk, goal, extra, emit):
        owners = [place[level * near + (spot ^ step)] for step in range(near)]

        @pl.loop(0, cuts[chunk] // 16)
        def _(tile):
            here = pl.ds(pl.multiple_of(tile * 16, 16), 16)
            there = pl.ds(pl.multiple_of(starts[chunk] + tile * 16, 16), 16)
            terms = [term[goal, spot, there, :].astype(jnp.float32)]
            terms += [arrived[chunk][goal, step - 1, here, :].astype(jnp.float32) for step in range(1, near)]
            for block in range(blocks):
                total = None
                for owner, value in zip(owners, terms):
                    part = jnp.where(owner == block, 1.0, 0.0) * value
                    total = part if total is None else total + part
                for ref in extra:
                    total = total + ref[block, here, :].astype(jnp.float32)
                emit(block, here, there, total)

    def await_near(chunk, goal):
        for step in range(1, near):
            sum_across(chunk, goal, step).wait_recv()

    def pass_on(chunk, left):
        def emit_to(target):
            def emit(block, here, there, total):
                target[block, here, :] = total.astype(target.dtype)
            return emit

        @pl.when(level + left < levels)
        def _():
            goal, target = level + left, to_up[chunk].at[left - 1]
            await_near(chunk, goal)
            if left < hops:
                @pl.when(level > 0)
                def _():
                    sum_up(chunk, left + 1).wait_recv()
                    sums(chunk, goal, [below[chunk].at[left]], emit_to(target))
            pl.when(level == 0)(lambda: sums(chunk, goal, [], emit_to(target)))
            sum_up(chunk, left).start()

        @pl.when(level >= left)
        def _():
            goal, target = level - left, to_down[chunk].at[left - 1]
            await_near(chunk, goal)
            if left < hops:
                @pl.when(level < levels - 1)
                def _():
                    sum_down(chunk, left + 1).wait_recv()
                    sums(chunk, goal, [above[chunk].at[left]], emit_to(target))
            pl.when(level == levels - 1)(lambda: sums(chunk, goal, [], emit_to(target)))
            sum_down(chunk, left).start()

    def up(chunk, hop):
        source = slabs[chunk] if hop == 0 else from_below[chunk * hops + hop - 1]
        return remote(source, from_below[chunk * hops + hop], up_send.at[chunk, hop],
                      up_recv.at[chunk, hop], "expert", me + near)

    def down(chunk, hop):
        source = slabs[chunk] if hop == 0 else from_above[chunk * hops + hop - 1]
        return remote(source, from_above[chunk * hops + hop], down_send.at[chunk, hop],
                      down_recv.at[chunk, hop], "expert", me - near)

    def across(chunk, origin, step):
        rows = pl.ds(starts[chunk], cuts[chunk])
        return remote(picked[chunk].at[origin, step - 1], out.at[:, origin, spot, rows],
                      near_send.at[chunk, origin, step - 1], near_recv.at[chunk, origin, step - 1],
                      "expert", level * near + (spot ^ step))

    def hand_on(chunk, origin, held):
        for step in range(1, near):
            picked[chunk][origin, step - 1] = held[place[level * near + (spot ^ step)]]
            across(chunk, origin, step).start()
        out[:, origin, spot, pl.ds(starts[chunk], cuts[chunk]), :] = held[place[me]]

    def settle(chunk):
        def emit(block, here, there, total):
            slabs[chunk][block, 0, here, :] = (
                beta_first * first[block, there, :] + (1.0 - beta_first) * total
            ).astype(out.dtype)
            slabs[chunk][block, 1, here, :] = (
                beta_second * second[block, there, :] + (1.0 - beta_second) * total * total
            ).astype(out.dtype)

        await_near(chunk, level)
        pl.when(level > 0)(lambda: sum_up(chunk, 1).wait_recv())
        pl.when(level < levels - 1)(lambda: sum_down(chunk, 1).wait_recv())
        under, over = below[chunk].at[0], above[chunk].at[0]
        pl.when(level == 0)(lambda: sums(chunk, level, [over], emit))
        pl.when(level == levels - 1)(lambda: sums(chunk, level, [under], emit))
        pl.when((level > 0) & (level < levels - 1))(lambda: sums(chunk, level, [under, over], emit))
        pl.when(level < levels - 1)(lambda: up(chunk, 0).start())
        pl.when(level > 0)(lambda: down(chunk, 0).start())
        hand_on(chunk, level, slabs[chunk])

    def forward(chunk, hop):
        @pl.when(level > hop)
        def _():
            up(chunk, hop).wait_recv()
            if hop < hops - 1:
                pl.when(level < levels - 1)(lambda: up(chunk, hop + 1).start())
            hand_on(chunk, level - hop - 1, from_below[chunk * hops + hop])

        @pl.when(level < levels - 1 - hop)
        def _():
            down(chunk, hop).wait_recv()
            if hop < hops - 1:
                pl.when(level > 0)(lambda: down(chunk, hop + 1).start())
            hand_on(chunk, level + hop + 1, from_above[chunk * hops + hop])

    for chunk in range(chunks):
        for left in range(hops, 0, -1):
            pl.when(level + left < levels)(lambda c=chunk, n=left: sum_start(c, level + n))
            pl.when(level >= left)(lambda c=chunk, n=left: sum_start(c, level - n))
        sum_start(chunk, level)

    def stages(chunk):
        return [functools.partial(pass_on, chunk, left) for left in range(hops, 0, -1)] + [
            functools.partial(settle, chunk)
        ]

    for stage in stages(0):
        stage()
    for chunk in range(chunks):
        coming = stages(chunk + 1) if chunk + 1 < chunks else []
        if coming:
            coming[0]()
        for hop in range(hops):
            if coming:
                coming[hop + 1]()
            forward(chunk, hop)

    for chunk in range(chunks):
        for left in range(1, levels):
            pl.when(level + left < levels)(lambda c=chunk, n=left: sum_up(c, n).wait_send())
            pl.when(level >= left)(lambda c=chunk, n=left: sum_down(c, n).wait_send())
        for hop in range(hops):
            pl.when((level < levels - 1) & (level >= hop))(lambda c=chunk, h=hop: up(c, h).wait_send())
            pl.when((level > 0) & (level < levels - hop))(lambda c=chunk, h=hop: down(c, h).wait_send())
        for goal in range(levels):
            for step in range(1, near):
                sum_across(chunk, goal, step).wait_send()
                across(chunk, goal, step).wait()


def in_vmem():
    return pl.BlockSpec(memory_space=pltpu.VMEM)


def in_smem():
    return pl.BlockSpec(memory_space=pltpu.SMEM)


def call_gather(placement, slab, levels, near, collective_id, tokens=None):
    channels, blocks, rows, cols = slab.shape
    kind = slab.dtype
    out_shape = [jax.ShapeDtypeStruct((channels, levels, near, rows, cols), kind)]
    in_specs = [in_smem(), in_vmem()]
    operands = [placement, slab]
    out_specs = [in_vmem()]
    dma = pltpu.SemaphoreType.DMA
    scratch = [pltpu.VMEM((blocks, rows, cols), kind)] * (2 * channels * (levels - 1))
    scratch += [pltpu.VMEM((channels, levels, near - 1, rows, cols), kind)]
    scratch += [dma((channels, levels - 1))] * 4 + [dma((channels, levels, near - 1))] * 2
    if tokens is not None:
        count, width = tokens.shape
        out_shape.append(jax.ShapeDtypeStruct((2, count, width // 2), tokens.dtype))
        in_specs.append(in_vmem())
        operands.append(tokens)
        out_specs.append(in_vmem())
        scratch += [dma, dma, dma]
    return pl.pallas_call(
        functools.partial(gather_kernel, channels, levels, near, tokens is not None),
        out_shape=out_shape, in_specs=in_specs, out_specs=out_specs, scratch_shapes=scratch,
        compiler_params=pltpu.CompilerParams(
            collective_id=collective_id, has_side_effects=True, vmem_limit_bytes=VMEM_BYTES
        ),
    )(*operands)


def call_update(placement, term, first, second, pieces, collective_id):
    levels, near, rows, cols = term.shape
    blocks = first.shape[0]
    kind = term.dtype
    tiles = rows // 16
    pieces = min(pieces, tiles)
    cuts = [16 * ((piece + 1) * tiles // pieces - piece * tiles // pieces) for piece in range(pieces)]
    hops = levels - 1
    dma = pltpu.SemaphoreType.DMA

    def each(make):
        return [pltpu.VMEM(make(cut), kind) for cut in cuts]

    scratch = each(lambda cut: (levels, near - 1, cut, cols))
    for _ in range(4):
        scratch += each(lambda cut: (hops, blocks, cut, cols))
    scratch += each(lambda cut: (blocks, 2, cut, cols))
    scratch += each(lambda cut: (levels, near - 1, 2, cut, cols))
    for _ in range(2):
        for cut in cuts:
            scratch += [pltpu.VMEM((blocks, 2, cut, cols), kind)] * hops
    scratch += [dma((pieces, hops))] * 4 + [dma((pieces, levels, near - 1))] * 2
    scratch += [dma((pieces, hops))] * 4 + [dma((pieces, levels, near - 1))] * 2
    return pl.pallas_call(
        functools.partial(update_kernel, levels, near, cuts),
        out_shape=jax.ShapeDtypeStruct((2, levels, near, rows, cols), kind),
        in_specs=[in_smem(), in_vmem(), in_vmem(), in_vmem()], out_specs=in_vmem(),
        scratch_shapes=scratch,
        compiler_params=pltpu.CompilerParams(
            collective_id=collective_id, has_side_effects=True, vmem_limit_bytes=VMEM_BYTES
        ),
    )(placement, term, first, second)


def on_device(weights, first_moment, second_moment, placement, block_counts, tokens, hidden_grad):
    expert_count = lax.axis_size("expert")
    dp_count = lax.axis_size("dp")
    block_total, span_rows, col_total = weights.shape
    row_total, model = tokens.shape[2:]
    near = plane_size(expert_count)
    levels = expert_count // near
    fits = dp_count == 2 and near > 1 and levels > 1 and levels * near == expert_count
    if not fits or span_rows % 16 or model % 256 or col_total % 128 or row_total % 16:
        return on_device_wide(
            weights, first_moment, second_moment, placement, block_counts, tokens, hidden_grad
        )
    part_rows = expert_count * span_rows
    core = lax.axis_index("dp")
    swap = [(0, 1), (1, 0)]
    live_mask = (jnp.arange(row_total) < BLOCK * block_counts[0, 0])[:, None]

    own_rows, inputs = call_gather(placement, weights[None], levels, near, 0, tokens[0, 0])
    own_rows = own_rows.reshape(part_rows, col_total)
    inputs = inputs.reshape(2 * row_total, model // 2)
    mine = lax.dynamic_slice_in_dim(inputs, core * row_total, row_total)
    others = lax.dynamic_slice_in_dim(inputs, (1 - core) * row_total, row_total)
    away = jnp.dot(others, own_rows, preferred_element_type=jnp.float32)
    away = lax.ppermute(away, "dp", swap)
    projected = jnp.dot(mine, own_rows, preferred_element_type=jnp.float32) + away
    grad_here = silu_grads(projected, hidden_grad[0, 0], live_mask)
    grad_away = lax.ppermute(grad_here, "dp", swap)
    down = (((0,), (0,)), ((), ()))
    ordered = jnp.where(core == 0, jnp.stack([grad_here, grad_away]), jnp.stack([grad_away, grad_here]))
    term = lax.dot_general(
        inputs, ordered.reshape(2 * row_total, col_total), down, preferred_element_type=jnp.float32
    ).astype(jnp.bfloat16)
    here = call_update(
        placement, term.reshape(levels, near, span_rows, col_total), first_moment, second_moment, PIECES, 1
    )
    here = here.reshape(2, part_rows, col_total).astype(jnp.float32)
    updated = new_params(own_rows, here[0], here[1])
    return (updated[None], here[0][None], here[1][None])


def solution(mesh):
    in_specs = (
        P(None, ("dp", "expert"), None),
        P(None, ("dp", "expert"), None),
        P(None, ("dp", "expert"), None),
        P(),
        P("dp", "expert"),
        P("dp", "expert", None, None),
        P("dp", "expert", None, None),
    )
    out_specs = (P("expert", "dp", None), P("expert", "dp", None), P("expert", "dp", None))
    return jax.shard_map(
        on_device, mesh=mesh, in_specs=in_specs, out_specs=out_specs, check_vma=False
    )
```

```python
import functools

import jax
import jax.numpy as jnp
from jax import lax
from jax.experimental import pallas as pl
from jax.experimental.pallas import tpu as pltpu
from jax.sharding import PartitionSpec as P

BLOCK = 128


beta_first = 0.9
beta_second = 0.95
learning_rate = 0.001
weight_decay = 0.1
adam_epsilon = 1e-08
adam_steps = 10.0


def silu_grads(projected, upstream, live_mask):
    half_width = projected.shape[1] // 2
    gate_part = projected[:, :half_width]
    upward = projected[:, half_width:]
    sigmoid_gate = jax.nn.sigmoid(gate_part)
    masked = jnp.where(live_mask, upstream.astype(jnp.float32), 0.0)
    grad_gate = masked * upward * sigmoid_gate * (1.0 + gate_part * (1.0 - sigmoid_gate))
    grad_upward = masked * gate_part * sigmoid_gate
    return jnp.concatenate([grad_gate, grad_upward], axis=1).astype(jnp.bfloat16)


def moments(first_moment, second_moment, gradient):
    moment_one = beta_first * first_moment + (1.0 - beta_first) * gradient
    moment_two = beta_second * second_moment + (1.0 - beta_second) * gradient * gradient
    return moment_one, moment_two


def new_params(params, moment_one, moment_two):
    correct_one = 1.0 - beta_first**adam_steps
    correct_two = 1.0 - beta_second**adam_steps
    params_full = params.astype(jnp.float32)
    step_size = (
        moment_one / correct_one / (jnp.sqrt(moment_two / correct_two) + adam_epsilon)
        + weight_decay * params_full
    )
    return (params_full - learning_rate * step_size).astype(jnp.bfloat16)


def exchange(x, axis):
    return lax.all_to_all(x, axis, split_axis=0, concat_axis=0, tiled=True)


def on_device_wide(weights, first_moment, second_moment, placement, block_counts, tokens, hidden_grad):
    expert_count = lax.axis_size("expert")
    dp_count = lax.axis_size("dp")
    block_total, span_rows, col_total = weights.shape
    row_total = tokens.shape[2]
    part_rows = expert_count * span_rows
    owner_table = (placement[:, None] == jnp.arange(block_total)[None, :]).astype(jnp.bfloat16)
    live_mask = (jnp.arange(row_total) < BLOCK * block_counts[0, 0])[:, None]

    own_rows = exchange(jnp.take(weights, placement, axis=0), "expert")
    own_rows = own_rows.reshape(part_rows, col_total)
    inputs = lax.all_to_all(tokens[0, 0], "dp", split_axis=1, concat_axis=0, tiled=True)
    partial = jnp.dot(inputs, own_rows, preferred_element_type=jnp.float32)
    projected = lax.psum_scatter(partial, "dp", scatter_dimension=0, tiled=True)
    grad_proj = silu_grads(projected, hidden_grad[0, 0], live_mask)
    grad_proj = lax.all_gather(grad_proj, "dp", axis=0, tiled=True)
    term = lax.dot_general(
        inputs, grad_proj, (((0,), (0,)), ((), ())), preferred_element_type=jnp.float32
    ).astype(jnp.bfloat16)
    at_home = exchange(term.reshape(expert_count, span_rows * col_total), "expert")
    block_grad = lax.dot_general(
        owner_table, at_home, (((0,), (0,)), ((), ())), preferred_element_type=jnp.float32
    ).reshape(block_total, span_rows, col_total)
    moment_one, moment_two = moments(first_moment, second_moment, block_grad)
    one_here = exchange(jnp.take(moment_one.astype(jnp.bfloat16), placement, axis=0), "expert")
    two_here = exchange(jnp.take(moment_two.astype(jnp.bfloat16), placement, axis=0), "expert")
    one_here = one_here.reshape(part_rows, col_total).astype(jnp.float32)
    two_here = two_here.reshape(part_rows, col_total).astype(jnp.float32)
    updated = new_params(own_rows, one_here, two_here)
    return (updated[None], one_here[None], two_here[None])


MESH = pl.DeviceIdType.MESH
VMEM_BYTES = 60 * 1024 * 1024
PIECES = 3
WEIGHT_PIECES = 2
LEAD = 1


def plane_size(expert_count):
    size = 1
    while 4 * size * size <= expert_count:
        size *= 2
    return size


def remote(source, target, send_sem, recv_sem, axis, index):
    return pltpu.make_async_remote_copy(
        src_ref=source, dst_ref=target, send_sem=send_sem, recv_sem=recv_sem,
        device_id={axis: index}, device_id_type=MESH,
    )


def greet(level, levels, near, me, with_dp):
    barrier = pltpu.get_barrier_semaphore()

    def signal(axis, index):
        pl.semaphore_signal(barrier, inc=1, device_id={axis: index}, device_id_type=MESH)

    for step in range(1, near):
        signal("expert", me - me % near + ((me % near) ^ step))
    if with_dp:
        signal("dp", 1 - lax.axis_index("dp"))
    pl.when(level > 0)(lambda: signal("expert", me - near))
    pl.when(level < levels - 1)(lambda: signal("expert", me + near))
    count = near - 1 + int(with_dp)
    pl.semaphore_wait(
        barrier, count + (level > 0).astype(jnp.int32) + (level < levels - 1).astype(jnp.int32)
    )


def gather_kernel(cuts, levels, near, with_tokens, *refs):
    channels = len(cuts)
    starts = [sum(cuts[:channel]) for channel in range(channels)]
    slots = channels * (levels - 1)
    fixed = 5 if with_tokens else 3
    from_below, from_above = refs[fixed:fixed + slots], refs[fixed + slots:fixed + 2 * slots]
    chosen = refs[fixed + 2 * slots:fixed + 2 * slots + channels]
    refs = refs[:fixed] + refs[fixed + 2 * slots + channels:]

    def rows(channel):
        return pl.ds(starts[channel], cuts[channel])

    def slot(channel, hop):
        return channel * (levels - 1) + hop

    if with_tokens:
        (place, slab, tokens, out, inputs,
         up_send, up_recv, down_send, down_recv, near_send, near_recv, dp_send, dp_recv, own_sem) = refs
    else:
        (place, slab, out,
         up_send, up_recv, down_send, down_recv, near_send, near_recv) = refs
    me = lax.axis_index("expert")
    level, spot = me // near, me % near
    greet(level, levels, near, me, with_tokens)

    def up(channel, hop):
        source = slab.at[:, rows(channel)] if hop == 0 else from_below[slot(channel, hop - 1)]
        return remote(source, from_below[slot(channel, hop)], up_send.at[channel, hop],
                      up_recv.at[channel, hop], "expert", me + near)

    def down(channel, hop):
        source = slab.at[:, rows(channel)] if hop == 0 else from_above[slot(channel, hop - 1)]
        return remote(source, from_above[slot(channel, hop)], down_send.at[channel, hop],
                      down_recv.at[channel, hop], "expert", me - near)

    def across(channel, origin, step):
        return remote(chosen[channel].at[origin, step - 1], out.at[origin, spot, rows(channel)],
                      near_send.at[channel, origin, step - 1], near_recv.at[channel, origin, step - 1],
                      "expert", level * near + (spot ^ step))

    def hand_on(channel, origin, held):
        for step in range(1, near):
            chosen[channel][origin, step - 1] = held[place[level * near + (spot ^ step)]]
            across(channel, origin, step).start()
        out[origin, spot, rows(channel), :] = held[place[me]]

    for channel in range(channels):
        pl.when(level < levels - 1)(lambda c=channel: up(c, 0).start())
        pl.when(level > 0)(lambda c=channel: down(c, 0).start())
    if with_tokens:
        core = lax.axis_index("dp")
        width = inputs.shape[2]
        other = 1 - core

        def columns(index):
            return tokens.at[:, pl.ds(pl.multiple_of(index * width, 128), width)]

        swap = remote(columns(other), inputs.at[core], dp_send, dp_recv, "dp", other)
        swap.start()
        keep = pltpu.make_async_copy(columns(core), inputs.at[core], own_sem)
        keep.start()
    for channel in range(channels):
        hand_on(channel, level, slab.at[:, rows(channel)])
    for hop in range(levels - 1):
        for channel in range(channels):

            @pl.when(level > hop)
            def _():
                up(channel, hop).wait_recv()
                if hop < levels - 2:
                    pl.when(level < levels - 1)(lambda: up(channel, hop + 1).start())
                hand_on(channel, level - hop - 1, from_below[slot(channel, hop)])

            @pl.when(level < levels - 1 - hop)
            def _():
                down(channel, hop).wait_recv()
                if hop < levels - 2:
                    pl.when(level > 0)(lambda: down(channel, hop + 1).start())
                hand_on(channel, level + hop + 1, from_above[slot(channel, hop)])

    for channel in range(channels):
        for hop in range(levels - 1):
            pl.when((level < levels - 1) & (level >= hop))(lambda c=channel, h=hop: up(c, h).wait_send())
            pl.when((level > 0) & (level < levels - hop))(lambda c=channel, h=hop: down(c, h).wait_send())
        for origin in range(levels):
            for step in range(1, near):
                across(channel, origin, step).wait()
    if with_tokens:
        swap.wait()
        keep.wait()


def update_kernel(levels, near, cuts, *refs):
    place, term, first, second, out = refs[:5]
    chunks, hops = len(cuts), levels - 1
    at = [5]

    def take(count):
        at[0] += count
        return refs[at[0] - count:at[0]]

    arrived, below, above, to_up, to_down, slabs, picked = (take(chunks) for _ in range(7))
    from_below, from_above = take(chunks * hops), take(chunks * hops)
    (sum_up_send, sum_up_recv, sum_down_send, sum_down_recv, sum_near_send, sum_near_recv,
     up_send, up_recv, down_send, down_recv, near_send, near_recv) = refs[at[0]:]
    me = lax.axis_index("expert")
    level, spot = me // near, me % near
    blocks, _, cols = first.shape
    starts = [sum(cuts[:chunk]) for chunk in range(chunks)]
    greet(level, levels, near, me, False)

    def sum_across(chunk, goal, step):
        rows = pl.ds(starts[chunk], cuts[chunk])
        return remote(term.at[goal, spot ^ step, rows], arrived[chunk].at[goal, step - 1],
                      sum_near_send.at[chunk, goal, step - 1], sum_near_recv.at[chunk, goal, step - 1],
                      "expert", level * near + (spot ^ step))

    def sum_up(chunk, left):
        return remote(to_up[chunk].at[left - 1], below[chunk].at[left - 1], sum_up_send.at[chunk, left - 1],
                      sum_up_recv.at[chunk, left - 1], "expert", me + near)

    def sum_down(chunk, left):
        return remote(to_down[chunk].at[left - 1], above[chunk].at[left - 1],
                      sum_down_send.at[chunk, left - 1], sum_down_recv.at[chunk, left - 1],
                      "expert", me - near)

    def sum_start(chunk, goal):
        for step in range(1, near):
            sum_across(chunk, goal, step).start()

    def sums(chunk, goal, extra, emit):
        owners = [place[level * near + (spot ^ step)] for step in range(near)]

        @pl.loop(0, cuts[chunk] // 16)
        def _(tile):
            here = pl.ds(pl.multiple_of(tile * 16, 16), 16)
            there = pl.ds(pl.multiple_of(starts[chunk] + tile * 16, 16), 16)
            terms = [term[goal, spot, there, :].astype(jnp.float32)]
            terms += [arrived[chunk][goal, step - 1, here, :].astype(jnp.float32) for step in range(1, near)]
            for block in range(blocks):
                total = None
                for owner, value in zip(owners, terms):
                    part = jnp.where(owner == block, 1.0, 0.0) * value
                    total = part if total is None else total + part
                for ref in extra:
                    total = total + ref[block, here, :].astype(jnp.float32)
                emit(block, here, there, total)

    def await_near(chunk, goal):
        for step in range(1, near):
            sum_across(chunk, goal, step).wait_recv()

    def pass_on(chunk, left):
        def emit_to(target):
            def emit(block, here, there, total):
                target[block, here, :] = total.astype(target.dtype)
            return emit

        @pl.when(level + left < levels)
        def _():
            goal, target = level + left, to_up[chunk].at[left - 1]
            await_near(chunk, goal)
            if left < hops:
                @pl.when(level > 0)
                def _():
                    sum_up(chunk, left + 1).wait_recv()
                    sums(chunk, goal, [below[chunk].at[left]], emit_to(target))
            pl.when(level == 0)(lambda: sums(chunk, goal, [], emit_to(target)))
            sum_up(chunk, left).start()

        @pl.when(level >= left)
        def _():
            goal, target = level - left, to_down[chunk].at[left - 1]
            await_near(chunk, goal)
            if left < hops:
                @pl.when(level < levels - 1)
                def _():
                    sum_down(chunk, left + 1).wait_recv()
                    sums(chunk, goal, [above[chunk].at[left]], emit_to(target))
            pl.when(level == levels - 1)(lambda: sums(chunk, goal, [], emit_to(target)))
            sum_down(chunk, left).start()

    def up(chunk, hop):
        source = slabs[chunk] if hop == 0 else from_below[chunk * hops + hop - 1]
        return remote(source, from_below[chunk * hops + hop], up_send.at[chunk, hop],
                      up_recv.at[chunk, hop], "expert", me + near)

    def down(chunk, hop):
        source = slabs[chunk] if hop == 0 else from_above[chunk * hops + hop - 1]
        return remote(source, from_above[chunk * hops + hop], down_send.at[chunk, hop],
                      down_recv.at[chunk, hop], "expert", me - near)

    def across(chunk, origin, step):
        rows = pl.ds(starts[chunk], cuts[chunk])
        return remote(picked[chunk].at[origin, step - 1], out.at[:, origin, spot, rows],
                      near_send.at[chunk, origin, step - 1], near_recv.at[chunk, origin, step - 1],
                      "expert", level * near + (spot ^ step))

    def hand_on(chunk, origin, held):
        for step in range(1, near):
            picked[chunk][origin, step - 1] = held[place[level * near + (spot ^ step)]]
            across(chunk, origin, step).start()
        out[:, origin, spot, pl.ds(starts[chunk], cuts[chunk]), :] = held[place[me]]

    def settle(chunk):
        def emit(block, here, there, total):
            slabs[chunk][block, 0, here, :] = (
                beta_first * first[block, there, :] + (1.0 - beta_first) * total
            ).astype(out.dtype)
            slabs[chunk][block, 1, here, :] = (
                beta_second * second[block, there, :] + (1.0 - beta_second) * total * total
            ).astype(out.dtype)

        await_near(chunk, level)
        pl.when(level > 0)(lambda: sum_up(chunk, 1).wait_recv())
        pl.when(level < levels - 1)(lambda: sum_down(chunk, 1).wait_recv())
        under, over = below[chunk].at[0], above[chunk].at[0]
        pl.when(level == 0)(lambda: sums(chunk, level, [over], emit))
        pl.when(level == levels - 1)(lambda: sums(chunk, level, [under], emit))
        pl.when((level > 0) & (level < levels - 1))(lambda: sums(chunk, level, [under, over], emit))
        pl.when(level < levels - 1)(lambda: up(chunk, 0).start())
        pl.when(level > 0)(lambda: down(chunk, 0).start())
        hand_on(chunk, level, slabs[chunk])

    def forward(chunk, hop):
        @pl.when(level > hop)
        def _():
            up(chunk, hop).wait_recv()
            if hop < hops - 1:
                pl.when(level < levels - 1)(lambda: up(chunk, hop + 1).start())
            hand_on(chunk, level - hop - 1, from_below[chunk * hops + hop])

        @pl.when(level < levels - 1 - hop)
        def _():
            down(chunk, hop).wait_recv()
            if hop < hops - 1:
                pl.when(level > 0)(lambda: down(chunk, hop + 1).start())
            hand_on(chunk, level + hop + 1, from_above[chunk * hops + hop])

    for chunk in range(chunks):
        for left in range(hops, 0, -1):
            pl.when(level + left < levels)(lambda c=chunk, n=left: sum_start(c, level + n))
            pl.when(level >= left)(lambda c=chunk, n=left: sum_start(c, level - n))
        sum_start(chunk, level)

    def stages(chunk):
        return [functools.partial(pass_on, chunk, left) for left in range(hops, 0, -1)] + [
            functools.partial(settle, chunk)
        ]

    for stage in stages(0):
        stage()
    for chunk in range(chunks):
        coming = stages(chunk + 1) if chunk + 1 < chunks else []
        for stage in coming[:LEAD]:
            stage()
        for hop in range(hops):
            for stage in coming[LEAD + hop:LEAD + hop + 1]:
                stage()
            forward(chunk, hop)
        for stage in coming[LEAD + hops:]:
            stage()

    for chunk in range(chunks):
        for left in range(1, levels):
            pl.when(level + left < levels)(lambda c=chunk, n=left: sum_up(c, n).wait_send())
            pl.when(level >= left)(lambda c=chunk, n=left: sum_down(c, n).wait_send())
        for hop in range(hops):
            pl.when((level < levels - 1) & (level >= hop))(lambda c=chunk, h=hop: up(c, h).wait_send())
            pl.when((level > 0) & (level < levels - hop))(lambda c=chunk, h=hop: down(c, h).wait_send())
        for goal in range(levels):
            for step in range(1, near):
                sum_across(chunk, goal, step).wait_send()
                across(chunk, goal, step).wait()


def cut_rows(rows, pieces):
    tiles = rows // 16
    pieces = min(pieces, tiles)
    return [16 * ((piece + 1) * tiles // pieces - piece * tiles // pieces) for piece in range(pieces)]


def in_vmem():
    return pl.BlockSpec(memory_space=pltpu.VMEM)


def in_smem():
    return pl.BlockSpec(memory_space=pltpu.SMEM)


def call_gather(placement, slab, levels, near, pieces, collective_id, tokens=None):
    blocks, rows, cols = slab.shape
    cuts = cut_rows(rows, pieces)
    channels = len(cuts)
    kind = slab.dtype
    out_shape = [jax.ShapeDtypeStruct((levels, near, rows, cols), kind)]
    in_specs = [in_smem(), in_vmem()]
    operands = [placement, slab]
    out_specs = [in_vmem()]
    dma = pltpu.SemaphoreType.DMA
    scratch = []
    for _ in range(2):
        for cut in cuts:
            scratch += [pltpu.VMEM((blocks, cut, cols), kind)] * (levels - 1)
    scratch += [pltpu.VMEM((levels, near - 1, cut, cols), kind) for cut in cuts]
    scratch += [dma((channels, levels - 1))] * 4 + [dma((channels, levels, near - 1))] * 2
    if tokens is not None:
        count, width = tokens.shape
        out_shape.append(jax.ShapeDtypeStruct((2, count, width // 2), tokens.dtype))
        in_specs.append(in_vmem())
        operands.append(tokens)
        out_specs.append(in_vmem())
        scratch += [dma, dma, dma]
    return pl.pallas_call(
        functools.partial(gather_kernel, cuts, levels, near, tokens is not None),
        out_shape=out_shape, in_specs=in_specs, out_specs=out_specs, scratch_shapes=scratch,
        compiler_params=pltpu.CompilerParams(
            collective_id=collective_id, has_side_effects=True, vmem_limit_bytes=VMEM_BYTES
        ),
    )(*operands)


def call_update(placement, term, first, second, pieces, collective_id):
    levels, near, rows, cols = term.shape
    blocks = first.shape[0]
    kind = term.dtype
    cuts = cut_rows(rows, pieces)
    pieces = len(cuts)
    hops = levels - 1
    dma = pltpu.SemaphoreType.DMA

    def each(make):
        return [pltpu.VMEM(make(cut), kind) for cut in cuts]

    scratch = each(lambda cut: (levels, near - 1, cut, cols))
    for _ in range(4):
        scratch += each(lambda cut: (hops, blocks, cut, cols))
    scratch += each(lambda cut: (blocks, 2, cut, cols))
    scratch += each(lambda cut: (levels, near - 1, 2, cut, cols))
    for _ in range(2):
        for cut in cuts:
            scratch += [pltpu.VMEM((blocks, 2, cut, cols), kind)] * hops
    scratch += [dma((pieces, hops))] * 4 + [dma((pieces, levels, near - 1))] * 2
    scratch += [dma((pieces, hops))] * 4 + [dma((pieces, levels, near - 1))] * 2
    return pl.pallas_call(
        functools.partial(update_kernel, levels, near, cuts),
        out_shape=jax.ShapeDtypeStruct((2, levels, near, rows, cols), kind),
        in_specs=[in_smem(), in_vmem(), in_vmem(), in_vmem()], out_specs=in_vmem(),
        scratch_shapes=scratch,
        compiler_params=pltpu.CompilerParams(
            collective_id=collective_id, has_side_effects=True, vmem_limit_bytes=VMEM_BYTES
        ),
    )(placement, term, first, second)


def on_device(weights, first_moment, second_moment, placement, block_counts, tokens, hidden_grad):
    expert_count = lax.axis_size("expert")
    dp_count = lax.axis_size("dp")
    block_total, span_rows, col_total = weights.shape
    row_total, model = tokens.shape[2:]
    near = plane_size(expert_count)
    levels = expert_count // near
    fits = dp_count == 2 and near > 1 and levels > 1 and levels * near == expert_count
    if not fits or span_rows % 16 or model % 256 or col_total % 128 or row_total % 16:
        return on_device_wide(
            weights, first_moment, second_moment, placement, block_counts, tokens, hidden_grad
        )
    part_rows = expert_count * span_rows
    core = lax.axis_index("dp")
    swap = [(0, 1), (1, 0)]
    live_mask = (jnp.arange(row_total) < BLOCK * block_counts[0, 0])[:, None]

    own_rows, inputs = call_gather(
        placement, weights, levels, near, WEIGHT_PIECES, 0, tokens[0, 0]
    )
    own_rows = own_rows.reshape(part_rows, col_total)
    inputs = inputs.reshape(2 * row_total, model // 2)
    mine = lax.dynamic_slice_in_dim(inputs, core * row_total, row_total)
    others = lax.dynamic_slice_in_dim(inputs, (1 - core) * row_total, row_total)
    away = jnp.dot(others, own_rows, preferred_element_type=jnp.float32)
    away = lax.ppermute(away, "dp", swap)
    projected = jnp.dot(mine, own_rows, preferred_element_type=jnp.float32) + away
    grad_here = silu_grads(projected, hidden_grad[0, 0], live_mask)
    grad_away = lax.ppermute(grad_here, "dp", swap)
    down = (((0,), (0,)), ((), ()))
    ordered = jnp.where(core == 0, jnp.stack([grad_here, grad_away]), jnp.stack([grad_away, grad_here]))
    term = lax.dot_general(
        inputs, ordered.reshape(2 * row_total, col_total), down, preferred_element_type=jnp.float32
    ).astype(jnp.bfloat16)
    here = call_update(
        placement, term.reshape(levels, near, span_rows, col_total), first_moment, second_moment, PIECES, 1
    )
    here = here.reshape(2, part_rows, col_total).astype(jnp.float32)
    updated = new_params(own_rows, here[0], here[1])
    return (updated[None], here[0][None], here[1][None])


def solution(mesh):
    in_specs = (
        P(None, ("dp", "expert"), None),
        P(None, ("dp", "expert"), None),
        P(None, ("dp", "expert"), None),
        P(),
        P("dp", "expert"),
        P("dp", "expert", None, None),
        P("dp", "expert", None, None),
    )
    out_specs = (P("expert", "dp", None), P("expert", "dp", None), P("expert", "dp", None))
    return jax.shard_map(
        on_device, mesh=mesh, in_specs=in_specs, out_specs=out_specs, check_vma=False
    )
```

```python
import functools

import jax
import jax.numpy as jnp
from jax import lax
from jax.experimental import pallas as pl
from jax.experimental.pallas import tpu as pltpu
from jax.sharding import PartitionSpec as P

BLOCK = 128


beta_first = 0.9
beta_second = 0.95
learning_rate = 0.001
weight_decay = 0.1
adam_epsilon = 1e-08
adam_steps = 10.0


def silu_grads(projected, upstream, live_mask):
    half_width = projected.shape[1] // 2
    gate_part = projected[:, :half_width]
    upward = projected[:, half_width:]
    sigmoid_gate = jax.nn.sigmoid(gate_part)
    masked = jnp.where(live_mask, upstream.astype(jnp.float32), 0.0)
    grad_gate = masked * upward * sigmoid_gate * (1.0 + gate_part * (1.0 - sigmoid_gate))
    grad_upward = masked * gate_part * sigmoid_gate
    return jnp.concatenate([grad_gate, grad_upward], axis=1).astype(jnp.bfloat16)


def moments(first_moment, second_moment, gradient):
    moment_one = beta_first * first_moment + (1.0 - beta_first) * gradient
    moment_two = beta_second * second_moment + (1.0 - beta_second) * gradient * gradient
    return moment_one, moment_two


def new_params(params, moment_one, moment_two):
    correct_one = 1.0 - beta_first**adam_steps
    correct_two = 1.0 - beta_second**adam_steps
    params_full = params.astype(jnp.float32)
    step_size = (
        moment_one / correct_one / (jnp.sqrt(moment_two / correct_two) + adam_epsilon)
        + weight_decay * params_full
    )
    return (params_full - learning_rate * step_size).astype(jnp.bfloat16)


def exchange(x, axis):
    return lax.all_to_all(x, axis, split_axis=0, concat_axis=0, tiled=True)


def on_device_wide(weights, first_moment, second_moment, placement, block_counts, tokens, hidden_grad):
    expert_count = lax.axis_size("expert")
    dp_count = lax.axis_size("dp")
    block_total, span_rows, col_total = weights.shape
    row_total = tokens.shape[2]
    part_rows = expert_count * span_rows
    owner_table = (placement[:, None] == jnp.arange(block_total)[None, :]).astype(jnp.bfloat16)
    live_mask = (jnp.arange(row_total) < BLOCK * block_counts[0, 0])[:, None]

    own_rows = exchange(jnp.take(weights, placement, axis=0), "expert")
    own_rows = own_rows.reshape(part_rows, col_total)
    inputs = lax.all_to_all(tokens[0, 0], "dp", split_axis=1, concat_axis=0, tiled=True)
    partial = jnp.dot(inputs, own_rows, preferred_element_type=jnp.float32)
    projected = lax.psum_scatter(partial, "dp", scatter_dimension=0, tiled=True)
    grad_proj = silu_grads(projected, hidden_grad[0, 0], live_mask)
    grad_proj = lax.all_gather(grad_proj, "dp", axis=0, tiled=True)
    term = lax.dot_general(
        inputs, grad_proj, (((0,), (0,)), ((), ())), preferred_element_type=jnp.float32
    ).astype(jnp.bfloat16)
    at_home = exchange(term.reshape(expert_count, span_rows * col_total), "expert")
    block_grad = lax.dot_general(
        owner_table, at_home, (((0,), (0,)), ((), ())), preferred_element_type=jnp.float32
    ).reshape(block_total, span_rows, col_total)
    moment_one, moment_two = moments(first_moment, second_moment, block_grad)
    one_here = exchange(jnp.take(moment_one.astype(jnp.bfloat16), placement, axis=0), "expert")
    two_here = exchange(jnp.take(moment_two.astype(jnp.bfloat16), placement, axis=0), "expert")
    one_here = one_here.reshape(part_rows, col_total).astype(jnp.float32)
    two_here = two_here.reshape(part_rows, col_total).astype(jnp.float32)
    updated = new_params(own_rows, one_here, two_here)
    return (updated[None], one_here[None], two_here[None])


MESH = pl.DeviceIdType.MESH
VMEM_BYTES = 60 * 1024 * 1024
PIECES = 3
WEIGHT_PIECES = 2
LEAD = 1


def plane_size(expert_count):
    size = 1
    while 4 * size * size <= expert_count:
        size *= 2
    return size


def remote(source, target, send_sem, recv_sem, axis, index):
    return pltpu.make_async_remote_copy(
        src_ref=source, dst_ref=target, send_sem=send_sem, recv_sem=recv_sem,
        device_id={axis: index}, device_id_type=MESH,
    )


def greet(level, levels, near, me, with_dp):
    barrier = pltpu.get_barrier_semaphore()

    def signal(axis, index):
        pl.semaphore_signal(barrier, inc=1, device_id={axis: index}, device_id_type=MESH)

    for step in range(1, near):
        signal("expert", me - me % near + ((me % near) ^ step))
    if with_dp:
        signal("dp", 1 - lax.axis_index("dp"))
    pl.when(level > 0)(lambda: signal("expert", me - near))
    pl.when(level < levels - 1)(lambda: signal("expert", me + near))
    count = near - 1 + int(with_dp)
    pl.semaphore_wait(
        barrier, count + (level > 0).astype(jnp.int32) + (level < levels - 1).astype(jnp.int32)
    )


def gather_kernel(cuts, levels, near, with_tokens, *refs):
    channels = len(cuts)
    starts = [sum(cuts[:channel]) for channel in range(channels)]
    slots = channels * (levels - 1)
    fixed = 5 if with_tokens else 3
    from_below, from_above = refs[fixed:fixed + slots], refs[fixed + slots:fixed + 2 * slots]
    chosen = refs[fixed + 2 * slots:fixed + 2 * slots + channels]
    refs = refs[:fixed] + refs[fixed + 2 * slots + channels:]

    def rows(channel):
        return pl.ds(starts[channel], cuts[channel])

    def slot(channel, hop):
        return channel * (levels - 1) + hop

    if with_tokens:
        (place, slab, tokens, out, inputs,
         up_send, up_recv, down_send, down_recv, near_send, near_recv, dp_send, dp_recv, own_sem) = refs
    else:
        (place, slab, out,
         up_send, up_recv, down_send, down_recv, near_send, near_recv) = refs
    me = lax.axis_index("expert")
    level, spot = me // near, me % near
    greet(level, levels, near, me, with_tokens)

    def up(channel, hop):
        source = slab.at[:, rows(channel)] if hop == 0 else from_below[slot(channel, hop - 1)]
        return remote(source, from_below[slot(channel, hop)], up_send.at[channel, hop],
                      up_recv.at[channel, hop], "expert", me + near)

    def down(channel, hop):
        source = slab.at[:, rows(channel)] if hop == 0 else from_above[slot(channel, hop - 1)]
        return remote(source, from_above[slot(channel, hop)], down_send.at[channel, hop],
                      down_recv.at[channel, hop], "expert", me - near)

    def across(channel, origin, step):
        return remote(chosen[channel].at[origin, step - 1], out.at[origin, spot, rows(channel)],
                      near_send.at[channel, origin, step - 1], near_recv.at[channel, origin, step - 1],
                      "expert", level * near + (spot ^ step))

    def hand_on(channel, origin, held):
        for step in range(1, near):
            chosen[channel][origin, step - 1] = held[place[level * near + (spot ^ step)]]
            across(channel, origin, step).start()
        out[origin, spot, rows(channel), :] = held[place[me]]

    for channel in range(channels):
        pl.when(level < levels - 1)(lambda c=channel: up(c, 0).start())
        pl.when(level > 0)(lambda c=channel: down(c, 0).start())
    if with_tokens:
        core = lax.axis_index("dp")
        width = inputs.shape[2]
        other = 1 - core

        def columns(index):
            return tokens.at[:, pl.ds(pl.multiple_of(index * width, 128), width)]

        swap = remote(columns(other), inputs.at[core], dp_send, dp_recv, "dp", other)
        swap.start()
        keep = pltpu.make_async_copy(columns(core), inputs.at[core], own_sem)
        keep.start()
    for channel in range(channels):
        hand_on(channel, level, slab.at[:, rows(channel)])
    for hop in range(levels - 1):
        for channel in range(channels):

            @pl.when(level > hop)
            def _():
                up(channel, hop).wait_recv()
                if hop < levels - 2:
                    pl.when(level < levels - 1)(lambda: up(channel, hop + 1).start())
                hand_on(channel, level - hop - 1, from_below[slot(channel, hop)])

            @pl.when(level < levels - 1 - hop)
            def _():
                down(channel, hop).wait_recv()
                if hop < levels - 2:
                    pl.when(level > 0)(lambda: down(channel, hop + 1).start())
                hand_on(channel, level + hop + 1, from_above[slot(channel, hop)])

    for channel in range(channels):
        for hop in range(levels - 1):
            pl.when((level < levels - 1) & (level >= hop))(lambda c=channel, h=hop: up(c, h).wait_send())
            pl.when((level > 0) & (level < levels - hop))(lambda c=channel, h=hop: down(c, h).wait_send())
        for origin in range(levels):
            for step in range(1, near):
                across(channel, origin, step).wait()
    if with_tokens:
        swap.wait()
        keep.wait()


def update_kernel(levels, near, cuts, *refs):
    place, term, first, second, out = refs[:5]
    chunks, hops = len(cuts), levels - 1
    at = [5]

    def take(count):
        at[0] += count
        return refs[at[0] - count:at[0]]

    arrived, below, above, to_up, to_down, slabs, picked = (take(chunks) for _ in range(7))
    from_below, from_above = take(chunks * hops), take(chunks * hops)
    (sum_up_send, sum_up_recv, sum_down_send, sum_down_recv, sum_near_send, sum_near_recv,
     up_send, up_recv, down_send, down_recv, near_send, near_recv) = refs[at[0]:]
    me = lax.axis_index("expert")
    level, spot = me // near, me % near
    blocks, _, cols = first.shape
    starts = [sum(cuts[:chunk]) for chunk in range(chunks)]
    greet(level, levels, near, me, False)

    def sum_across(chunk, goal, step):
        rows = pl.ds(starts[chunk], cuts[chunk])
        return remote(term.at[goal, spot ^ step, rows], arrived[chunk].at[goal, step - 1],
                      sum_near_send.at[chunk, goal, step - 1], sum_near_recv.at[chunk, goal, step - 1],
                      "expert", level * near + (spot ^ step))

    def sum_up(chunk, left):
        return remote(to_up[chunk].at[left - 1], below[chunk].at[left - 1], sum_up_send.at[chunk, left - 1],
                      sum_up_recv.at[chunk, left - 1], "expert", me + near)

    def sum_down(chunk, left):
        return remote(to_down[chunk].at[left - 1], above[chunk].at[left - 1],
                      sum_down_send.at[chunk, left - 1], sum_down_recv.at[chunk, left - 1],
                      "expert", me - near)

    def sum_start(chunk, goal):
        for step in range(1, near):
            sum_across(chunk, goal, step).start()

    def sums(chunk, goal, extra, emit):
        owners = [place[level * near + (spot ^ step)] for step in range(near)]

        @pl.loop(0, cuts[chunk] // 16)
        def _(tile):
            here = pl.ds(pl.multiple_of(tile * 16, 16), 16)
            there = pl.ds(pl.multiple_of(starts[chunk] + tile * 16, 16), 16)
            terms = [term[goal, spot, there, :].astype(jnp.float32)]
            terms += [arrived[chunk][goal, step - 1, here, :].astype(jnp.float32) for step in range(1, near)]
            for block in range(blocks):
                total = None
                for owner, value in zip(owners, terms):
                    part = jnp.where(owner == block, 1.0, 0.0) * value
                    total = part if total is None else total + part
                for ref in extra:
                    total = total + ref[block, here, :].astype(jnp.float32)
                emit(block, here, there, total)

    def await_near(chunk, goal):
        for step in range(1, near):
            sum_across(chunk, goal, step).wait_recv()

    def pass_on(chunk, left):
        def emit_to(target):
            def emit(block, here, there, total):
                target[block, here, :] = total.astype(target.dtype)
            return emit

        @pl.when(level + left < levels)
        def _():
            goal, target = level + left, to_up[chunk].at[left - 1]
            await_near(chunk, goal)
            if left < hops:
                @pl.when(level > 0)
                def _():
                    sum_up(chunk, left + 1).wait_recv()
                    sums(chunk, goal, [below[chunk].at[left]], emit_to(target))
            pl.when(level == 0)(lambda: sums(chunk, goal, [], emit_to(target)))
            sum_up(chunk, left).start()

        @pl.when(level >= left)
        def _():
            goal, target = level - left, to_down[chunk].at[left - 1]
            await_near(chunk, goal)
            if left < hops:
                @pl.when(level < levels - 1)
                def _():
                    sum_down(chunk, left + 1).wait_recv()
                    sums(chunk, goal, [above[chunk].at[left]], emit_to(target))
            pl.when(level == levels - 1)(lambda: sums(chunk, goal, [], emit_to(target)))
            sum_down(chunk, left).start()

    def up(chunk, hop):
        source = slabs[chunk] if hop == 0 else from_below[chunk * hops + hop - 1]
        return remote(source, from_below[chunk * hops + hop], up_send.at[chunk, hop],
                      up_recv.at[chunk, hop], "expert", me + near)

    def down(chunk, hop):
        source = slabs[chunk] if hop == 0 else from_above[chunk * hops + hop - 1]
        return remote(source, from_above[chunk * hops + hop], down_send.at[chunk, hop],
                      down_recv.at[chunk, hop], "expert", me - near)

    def across(chunk, origin, step):
        rows = pl.ds(starts[chunk], cuts[chunk])
        return remote(picked[chunk].at[origin, step - 1], out.at[:, origin, spot, rows],
                      near_send.at[chunk, origin, step - 1], near_recv.at[chunk, origin, step - 1],
                      "expert", level * near + (spot ^ step))

    def hand_on(chunk, origin, held):
        for step in range(1, near):
            picked[chunk][origin, step - 1] = held[place[level * near + (spot ^ step)]]
            across(chunk, origin, step).start()
        out[:, origin, spot, pl.ds(starts[chunk], cuts[chunk]), :] = held[place[me]]

    def settle(chunk):
        def emit(block, here, there, total):
            slabs[chunk][block, 0, here, :] = (
                beta_first * first[block, there, :] + (1.0 - beta_first) * total
            ).astype(out.dtype)
            slabs[chunk][block, 1, here, :] = (
                beta_second * second[block, there, :] + (1.0 - beta_second) * total * total
            ).astype(out.dtype)

        await_near(chunk, level)
        pl.when(level > 0)(lambda: sum_up(chunk, 1).wait_recv())
        pl.when(level < levels - 1)(lambda: sum_down(chunk, 1).wait_recv())
        under, over = below[chunk].at[0], above[chunk].at[0]
        pl.when(level == 0)(lambda: sums(chunk, level, [over], emit))
        pl.when(level == levels - 1)(lambda: sums(chunk, level, [under], emit))
        pl.when((level > 0) & (level < levels - 1))(lambda: sums(chunk, level, [under, over], emit))
        pl.when(level < levels - 1)(lambda: up(chunk, 0).start())
        pl.when(level > 0)(lambda: down(chunk, 0).start())
        hand_on(chunk, level, slabs[chunk])

    def forward(chunk, hop):
        @pl.when(level > hop)
        def _():
            up(chunk, hop).wait_recv()
            if hop < hops - 1:
                pl.when(level < levels - 1)(lambda: up(chunk, hop + 1).start())
            hand_on(chunk, level - hop - 1, from_below[chunk * hops + hop])

        @pl.when(level < levels - 1 - hop)
        def _():
            down(chunk, hop).wait_recv()
            if hop < hops - 1:
                pl.when(level > 0)(lambda: down(chunk, hop + 1).start())
            hand_on(chunk, level + hop + 1, from_above[chunk * hops + hop])

    for chunk in range(chunks):
        for left in range(hops, 0, -1):
            pl.when(level + left < levels)(lambda c=chunk, n=left: sum_start(c, level + n))
            pl.when(level >= left)(lambda c=chunk, n=left: sum_start(c, level - n))
        sum_start(chunk, level)

    def stages(chunk):
        return [functools.partial(pass_on, chunk, left) for left in range(hops, 0, -1)] + [
            functools.partial(settle, chunk)
        ]

    for stage in stages(0):
        stage()
    for chunk in range(chunks):
        coming = stages(chunk + 1) if chunk + 1 < chunks else []
        for stage in coming[:LEAD]:
            stage()
        for hop in range(hops):
            for stage in coming[LEAD + hop:LEAD + hop + 1]:
                stage()
            forward(chunk, hop)
        for stage in coming[LEAD + hops:]:
            stage()

    for chunk in range(chunks):
        for left in range(1, levels):
            pl.when(level + left < levels)(lambda c=chunk, n=left: sum_up(c, n).wait_send())
            pl.when(level >= left)(lambda c=chunk, n=left: sum_down(c, n).wait_send())
        for hop in range(hops):
            pl.when((level < levels - 1) & (level >= hop))(lambda c=chunk, h=hop: up(c, h).wait_send())
            pl.when((level > 0) & (level < levels - hop))(lambda c=chunk, h=hop: down(c, h).wait_send())
        for goal in range(levels):
            for step in range(1, near):
                sum_across(chunk, goal, step).wait_send()
                across(chunk, goal, step).wait()


def cut_rows(rows, pieces):
    tiles = rows // 16
    pieces = min(pieces, tiles)
    fullest = sorted(range(pieces), key=lambda piece: (piece == pieces - 1, piece == 0))
    extra = fullest[: tiles % pieces]
    return [16 * (tiles // pieces + int(piece in extra)) for piece in range(pieces)]


def in_vmem():
    return pl.BlockSpec(memory_space=pltpu.VMEM)


def in_smem():
    return pl.BlockSpec(memory_space=pltpu.SMEM)


def call_gather(placement, slab, levels, near, pieces, collective_id, tokens=None):
    blocks, rows, cols = slab.shape
    cuts = cut_rows(rows, pieces)
    channels = len(cuts)
    kind = slab.dtype
    out_shape = [jax.ShapeDtypeStruct((levels, near, rows, cols), kind)]
    in_specs = [in_smem(), in_vmem()]
    operands = [placement, slab]
    out_specs = [in_vmem()]
    dma = pltpu.SemaphoreType.DMA
    scratch = []
    for _ in range(2):
        for cut in cuts:
            scratch += [pltpu.VMEM((blocks, cut, cols), kind)] * (levels - 1)
    scratch += [pltpu.VMEM((levels, near - 1, cut, cols), kind) for cut in cuts]
    scratch += [dma((channels, levels - 1))] * 4 + [dma((channels, levels, near - 1))] * 2
    if tokens is not None:
        count, width = tokens.shape
        out_shape.append(jax.ShapeDtypeStruct((2, count, width // 2), tokens.dtype))
        in_specs.append(in_vmem())
        operands.append(tokens)
        out_specs.append(in_vmem())
        scratch += [dma, dma, dma]
    return pl.pallas_call(
        functools.partial(gather_kernel, cuts, levels, near, tokens is not None),
        out_shape=out_shape, in_specs=in_specs, out_specs=out_specs, scratch_shapes=scratch,
        compiler_params=pltpu.CompilerParams(
            collective_id=collective_id, has_side_effects=True, vmem_limit_bytes=VMEM_BYTES
        ),
    )(*operands)


def call_update(placement, term, first, second, pieces, collective_id):
    levels, near, rows, cols = term.shape
    blocks = first.shape[0]
    kind = term.dtype
    cuts = cut_rows(rows, pieces)
    pieces = len(cuts)
    hops = levels - 1
    dma = pltpu.SemaphoreType.DMA

    def each(make):
        return [pltpu.VMEM(make(cut), kind) for cut in cuts]

    scratch = each(lambda cut: (levels, near - 1, cut, cols))
    for _ in range(4):
        scratch += each(lambda cut: (hops, blocks, cut, cols))
    scratch += each(lambda cut: (blocks, 2, cut, cols))
    scratch += each(lambda cut: (levels, near - 1, 2, cut, cols))
    for _ in range(2):
        for cut in cuts:
            scratch += [pltpu.VMEM((blocks, 2, cut, cols), kind)] * hops
    scratch += [dma((pieces, hops))] * 4 + [dma((pieces, levels, near - 1))] * 2
    scratch += [dma((pieces, hops))] * 4 + [dma((pieces, levels, near - 1))] * 2
    return pl.pallas_call(
        functools.partial(update_kernel, levels, near, cuts),
        out_shape=jax.ShapeDtypeStruct((2, levels, near, rows, cols), kind),
        in_specs=[in_smem(), in_vmem(), in_vmem(), in_vmem()], out_specs=in_vmem(),
        scratch_shapes=scratch,
        compiler_params=pltpu.CompilerParams(
            collective_id=collective_id, has_side_effects=True, vmem_limit_bytes=VMEM_BYTES
        ),
    )(placement, term, first, second)


def on_device(weights, first_moment, second_moment, placement, block_counts, tokens, hidden_grad):
    expert_count = lax.axis_size("expert")
    dp_count = lax.axis_size("dp")
    block_total, span_rows, col_total = weights.shape
    row_total, model = tokens.shape[2:]
    near = plane_size(expert_count)
    levels = expert_count // near
    fits = dp_count == 2 and near > 1 and levels > 1 and levels * near == expert_count
    if not fits or span_rows % 16 or model % 256 or col_total % 128 or row_total % 16:
        return on_device_wide(
            weights, first_moment, second_moment, placement, block_counts, tokens, hidden_grad
        )
    part_rows = expert_count * span_rows
    core = lax.axis_index("dp")
    swap = [(0, 1), (1, 0)]
    live_mask = (jnp.arange(row_total) < BLOCK * block_counts[0, 0])[:, None]

    own_rows, inputs = call_gather(
        placement, weights, levels, near, WEIGHT_PIECES, 0, tokens[0, 0]
    )
    own_rows = own_rows.reshape(part_rows, col_total)
    inputs = inputs.reshape(2 * row_total, model // 2)
    mine = lax.dynamic_slice_in_dim(inputs, core * row_total, row_total)
    others = lax.dynamic_slice_in_dim(inputs, (1 - core) * row_total, row_total)
    away = jnp.dot(others, own_rows, preferred_element_type=jnp.float32)
    away = lax.ppermute(away, "dp", swap)
    projected = jnp.dot(mine, own_rows, preferred_element_type=jnp.float32) + away
    grad_here = silu_grads(projected, hidden_grad[0, 0], live_mask)
    grad_away = lax.ppermute(grad_here, "dp", swap)
    down = (((0,), (0,)), ((), ()))
    ordered = jnp.where(core == 0, jnp.stack([grad_here, grad_away]), jnp.stack([grad_away, grad_here]))
    term = lax.dot_general(
        inputs, ordered.reshape(2 * row_total, col_total), down, preferred_element_type=jnp.float32
    ).astype(jnp.bfloat16)
    here = call_update(
        placement, term.reshape(levels, near, span_rows, col_total), first_moment, second_moment, PIECES, 1
    )
    here = here.reshape(2, part_rows, col_total).astype(jnp.float32)
    updated = new_params(own_rows, here[0], here[1])
    return (updated[None], here[0][None], here[1][None])


def solution(mesh):
    in_specs = (
        P(None, ("dp", "expert"), None),
        P(None, ("dp", "expert"), None),
        P(None, ("dp", "expert"), None),
        P(),
        P("dp", "expert"),
        P("dp", "expert", None, None),
        P("dp", "expert", None, None),
    )
    out_specs = (P("expert", "dp", None), P("expert", "dp", None), P("expert", "dp", None))
    return jax.shard_map(
        on_device, mesh=mesh, in_specs=in_specs, out_specs=out_specs, check_vma=False
    )
```
